256 devices in a mesh: lat: 32 (over z_lo, y, core), ha: 8 (over x, z_hi).
Axes of the slice: x: 4, y: 4, z: 8 (z_hi: 2, z_lo: 4; z = z_hi * 4 + z_lo), core: 2. Of those that a mesh axis runs over, the one named last changes fastest.
Arguments:
- adjoint_e: float32 [3, 32, 2048, 128], P(None, 'ha', 'lat'), may hold values from -6 to 6
- adjoint_h: float32 [3, 32, 2048, 128], P(None, 'ha', 'lat'), may hold values from -6 to 6
- saved_e: bfloat16 [2, 3, 32, 2048, 128], P(None, None, 'ha', 'lat'), may hold values from -5 to 5
- labels: int32 [32, 2048, 128], P('ha', 'lat'), may hold values from 0 to 3
- eps_table: float32 [4], replicated, may hold values from 1 to 12
- chi_table: float32 [4], replicated, may hold values from 0.05 to 0.5
- density: float32 [2048, 128], P('lat'), may hold values from 0 to 1
- mon_cells: int32 [131072], P(('lat', 'ha')), may hold values from 0 to 32767
- mon_weight: float32 [131072], P(('lat', 'ha')), may hold values from 0.25 to 6.75
Outputs:
- final_e: float32 [3, 32, 2048, 128], P(None, 'ha', 'lat')
- final_h: float32 [3, 32, 2048, 128], P(None, 'ha', 'lat')
- design_grad: float32 [2048, 128], P('lat')
The draws below stay inside these ranges and needn't reach their ends.
Inputs may be any that keep to these rules, and one draw needn't show every extreme that they name: `labels`: label 0 marks design cells. `mon_cells`: entry m names a cell of the block of block number m // 512 (lat major, ha minor), numbered in z, x, y order within the block; entries may repeat.
All inputs are finite; a program needn't handle non-finite values.
Results may differ from the reference program's by a relative error of at most 0.0003.
Values sent between devices are 32-bit elements; how exact they have to be, the bound alone decides.
No kernel may reach another device: no remote copies, remote signals or barrier semaphores. Data moves between devices by JAX's collectives and lax.ppermute only.
A program may use at most 64 MiB of HBM per device.

```python
import jax
import jax.numpy as jnp
from jax import lax

CX = 64
CZ = 4
NY = 128
STEPS = 2
NREG = 4
MON_DEV = 512
RADIUS = 16
NX = 2048
NZ = 32
MON_ALL = 131072
N_HA = 8


def draw_mon_weight(key, part):
    position = jnp.arange(MON_ALL, dtype=jnp.float32) / MON_ALL
    base = jax.random.uniform(key, (MON_ALL,), jnp.float32, 0.5, 1.5)
    return base * (1.0 + 2.0 * position)


def plant(values, stream_key, smallest, top_value):
    longest = values.shape.index(max(values.shape))
    spots = []
    for shift in (0, 1):
        where = [jax.random.randint(jax.random.fold_in(stream_key, axis), (), 0, length) for axis, length in enumerate(values.shape)]
        where[longest] = (where[longest] + shift) % values.shape[longest]
        spots.append(tuple(where))
    return values.at[spots[0]].set(smallest).at[spots[1]].set(top_value)


def level_of(own_key, dims, split, smallest, high):
    gain, own = 1.0, jax.random.fold_in(own_key, 6)
    for dim, parts in split:
        heights = jnp.exp(jax.random.uniform(jax.random.fold_in(own, dim), (parts,), jnp.float32, smallest / len(split), high / len(split)))
        gain = gain * jnp.repeat(heights, dims[dim] // parts).reshape([-1 if axis == dim else 1 for axis in range(len(dims))])
    return gain


def centred(own_key, extent, scale, most, split=(), kind=jnp.bfloat16):
    factor_of = level_of(own_key, extent, split, -0.22, 0.18) if split else 1.0
    result = jax.random.normal(own_key, extent, jnp.float32) * scale * factor_of
    return jnp.minimum(jnp.maximum(result, -most), most).astype(kind)


def setup_inputs(seed: int = 0) -> dict:
    splits = jax.random.split(jax.random.key(seed), 10)
    adjoint_e = centred(splits[0], (3, NZ, NX, NY), 1.0, 6.0, ((1, 8), (2, 32)), jnp.float32)
    adjoint_h = centred(splits[1], (3, NZ, NX, NY), 1.0, 6.0, ((1, 8), (2, 32)), jnp.float32)
    saved_e = centred(splits[2], (STEPS, 3, NZ, NX, NY), 1.0, 5.0, ((2, 8), (3, 32)))
    labels = plant(jax.random.randint(splits[3], (NZ, NX, NY), 0, NREG), jax.random.fold_in(splits[3], 1), 0, NREG - 1).astype(jnp.int32)
    eps_table = jnp.clip(jax.random.uniform(splits[4], (NREG,), jnp.float32, 1.0, 12.0), 1.0, 12.0)
    chi_table = jnp.clip(jax.random.uniform(splits[5], (NREG,), jnp.float32, 0.05, 0.5), 0.05, 0.5)
    density = jnp.clip(1.0 * jax.random.uniform(splits[6], (NX, NY), jnp.float32) ** level_of(splits[6], (NX, NY), ((0, 32),), -0.2, 0.2), 0.0, 1.0)
    mon_cells = plant(jax.random.randint(splits[7], (MON_ALL,), 0, CZ * CX * NY), jax.random.fold_in(splits[7], 1), 0, (CZ * CX * NY) - 1).astype(jnp.int32)
    mon_weight = draw_mon_weight(jax.random.fold_in(splits[9], 71), 0)
    return dict(adjoint_e=adjoint_e, adjoint_h=adjoint_h, saved_e=saved_e, labels=labels, eps_table=eps_table, chi_table=chi_table, density=density, mon_cells=mon_cells, mon_weight=mon_weight)


sharpness = 8.0
threshold = 0.5
time_step = 0.5
epsilon = 1e-5


def lower(field, axis):
    length = field.shape[axis]
    first = jnp.zeros_like(lax.slice_in_dim(field, 0, 1, axis=axis))
    return jnp.concatenate([first, lax.slice_in_dim(field, 0, length - 1, axis=axis)], axis)


def upper(field, axis):
    length = field.shape[axis]
    last = jnp.zeros_like(lax.slice_in_dim(field, 0, 1, axis=axis))
    return jnp.concatenate([lax.slice_in_dim(field, 1, length, axis=axis), last], axis)


def curl_lower(field):
    field_x, field_y, field_z = field[0], field[1], field[2]
    curl_x = (field_z - lower(field_z, 2)) - (field_y - lower(field_y, 0))
    curl_y = (field_x - lower(field_x, 0)) - (field_z - lower(field_z, 1))
    curl_z = (field_y - lower(field_y, 1)) - (field_x - lower(field_x, 2))
    return jnp.stack([curl_x, curl_y, curl_z])


def curl_upper(field):
    field_x, field_y, field_z = field[0], field[1], field[2]
    curl_x = (upper(field_z, 2) - field_z) - (upper(field_y, 0) - field_y)
    curl_y = (upper(field_x, 0) - field_x) - (upper(field_z, 1) - field_z)
    curl_z = (upper(field_y, 1) - field_y) - (upper(field_x, 2) - field_x)
    return jnp.stack([curl_x, curl_y, curl_z])


def smooth_axis(field, axis):
    widths = [(0, 0), (0, 0)]
    widths[axis] = (RADIUS, RADIUS)
    padded = jnp.pad(field, widths)
    total = jnp.zeros_like(field)
    for position in range(2 * RADIUS + 1):
        weight = (RADIUS + 1 - abs(position - RADIUS)) / (RADIUS + 1) ** 2
        total = total + weight * lax.slice_in_dim(padded, position, position + field.shape[axis], axis=axis)
    return total


def smooth(field):
    return smooth_axis(smooth_axis(field, 1), 0)


def reference(adjoint_e, adjoint_h, saved_e, labels, eps_table, chi_table, density, mon_cells, mon_weight):
    eps_cell = eps_table[labels]
    chi_cell = chi_table[labels]
    design = (labels == 0).astype(jnp.float32)
    block = jnp.arange(MON_ALL, dtype=jnp.int32) // MON_DEV
    lat_index = block // N_HA
    ha_index = block % N_HA
    depth = mon_cells // (CX * NY)
    across = (mon_cells // NY) % CX
    column = mon_cells % NY
    flat = (((ha_index * CZ + depth) * NX + lat_index * CX + across) * NY + column).astype(jnp.int32)
    shape = adjoint_e.shape
    lam_e = adjoint_e
    lam_h = adjoint_h
    plane = jnp.zeros((NX, NY), jnp.float32)
    for index in reversed(range(STEPS)):
        forward = saved_e[index].astype(jnp.float32)
        jacobian = eps_cell[None] + 3.0 * chi_cell[None] * forward * forward
        picked = forward.reshape(3, -1)[:, flat]
        power = jnp.sum(mon_weight * jnp.sum(picked * picked, 0)) / MON_ALL + epsilon
        lam_e = lam_e.reshape(3, -1).at[:, flat].add(mon_weight * picked / power).reshape(shape)
        scaled = lam_e / jacobian
        plane = plane + jnp.sum(design * jnp.sum(scaled * forward, 0), 0)
        lam_h = lam_h - time_step * curl_lower(scaled)
        lam_e = lam_e + time_step * curl_upper(lam_h)
    filtered = smooth(density)
    slope = jnp.tanh(sharpness * (filtered - threshold))
    derivative = sharpness * (1.0 - slope * slope) / (jnp.tanh(sharpness * threshold) + jnp.tanh(sharpness * (1.0 - threshold)))
    design_grad = smooth(derivative * plane)
    return lam_e, lam_h, design_grad
```

```python
import jax
import jax.numpy as jnp
from jax import lax
from jax.experimental import pallas as pl
from jax.experimental.pallas import tpu as pltpu
from jax.sharding import PartitionSpec as P

RADIUS = 16
PAD = 8

sharpness = 8.0
threshold = 0.5
time_step = 0.5
epsilon = 1e-05

F32 = jnp.float32
VMEM = pl.BlockSpec(memory_space=pltpu.VMEM)
SMEM = pl.BlockSpec(memory_space=pltpu.SMEM)


def shifted(value, axis, steps):
    count = lax.axis_size(axis)
    return lax.ppermute(
        value, axis, [(i, i + steps) for i in range(count) if 0 <= i + steps < count]
    )


def lower_y(v):
    lane = lax.broadcasted_iota(jnp.int32, v.shape, 1)
    return jnp.where(lane == 0, 0.0, pltpu.roll(v, 1, 1))


def upper_y(v):
    lane = lax.broadcasted_iota(jnp.int32, v.shape, 1)
    last = v.shape[1] - 1
    return jnp.where(lane == last, 0.0, pltpu.roll(v, last, 1))


def lower_x(v):
    return pltpu.roll(v, 1, 0)


def upper_x(v):
    return pltpu.roll(v, v.shape[0] - 1, 0)


def smooth(padded, rows):
    cols = padded.shape[1]
    tall = padded.shape[0]

    def cone(offset):
        return jnp.maximum(RADIUS + 1 - jnp.abs(offset), 0).astype(F32)

    a = lax.broadcasted_iota(jnp.int32, (cols, cols), 0)
    b = lax.broadcasted_iota(jnp.int32, (cols, cols), 1)
    across = jnp.dot(
        padded, cone(a - b), precision=lax.Precision.HIGHEST, preferred_element_type=F32
    )
    r = lax.broadcasted_iota(jnp.int32, (rows, tall), 0)
    s = lax.broadcasted_iota(jnp.int32, (rows, tall), 1)
    down = jnp.dot(
        cone(s - RADIUS - r), across, precision=lax.Precision.HIGHEST, preferred_element_type=F32
    )
    return down * (1.0 / (RADIUS + 1) ** 4)


def prepare_kernel(e, h, sv, labels, density, cells, weight, w_out, power_out, nxt, prv):
    cz, cx, ny = labels.shape
    count = cells.shape[1]
    cell = cells[...]
    row = cell // ny
    col = cell % ny
    rows_hot = jnp.where(
        lax.broadcasted_iota(jnp.int32, (cz * cx, count), 0) == row, weight[...], 0.0
    )
    cols_hot = (lax.broadcasted_iota(jnp.int32, (ny, count), 0) == col).astype(F32)
    w = lax.dot_general(
        rows_hot,
        cols_hot,
        (((1,), (1,)), ((), ())),
        precision=lax.Precision.HIGHEST,
        preferred_element_type=F32,
    ).reshape(cz, cx, ny)
    w_out[...] = w
    steps = sv.shape[0]
    lane = lax.broadcasted_iota(jnp.int32, (1, ny), 1)
    packed = jnp.zeros((1, ny), F32)
    for k in range(steps):
        total = jnp.zeros((cx, ny), F32)
        for z in range(cz):
            square = jnp.zeros((cx, ny), F32)
            for c in range(3):
                f = sv[k, c, z].astype(F32)
                square = square + f * f
                slot = (1 + 2 * (steps - 1 - k)) * 3 * cz + c * cz + z
                nxt[slot] = f[cx - PAD :]
                prv[slot] = f[:PAD]
            total = total + w[z] * square
        packed = jnp.where(lane == k, jnp.sum(total), packed)
    power_out[...] = packed
    for c in range(3):
        for z in range(cz):
            nxt[c * cz + z] = e[c, z, cx - PAD :]
            prv[c * cz + z] = e[c, z, :PAD]
            nxt[(6 + c) * cz + z] = h[c, z, cx - PAD :]
            prv[(6 + c) * cz + z] = h[c, z, :PAD]
    for z in range(cz):
        nxt[12 * cz + z] = labels[z, cx - PAD :].astype(F32)
        prv[12 * cz + z] = labels[z, :PAD].astype(F32)
        nxt[13 * cz + z] = w[z, cx - PAD :]
        prv[13 * cz + z] = w[z, :PAD]
    for t in range(RADIUS // PAD):
        nxt[14 * cz + t] = density[cx - RADIUS + t * PAD : cx - RADIUS + (t + 1) * PAD]
        prv[14 * cz + t] = density[t * PAD : (t + 1) * PAD]


def region(labels, lo, hi, eps_t, chi_t, z, cz):
    lab = jnp.concatenate([lo[12 * cz + z], labels[z].astype(F32), hi[12 * cz + z]], 0)
    eps = jnp.full(lab.shape, eps_t[0], F32)
    chi = jnp.full(lab.shape, 3.0 * chi_t[0], F32)
    for r in range(1, eps_t.shape[0]):
        eps = jnp.where(lab == float(r), eps_t[r], eps)
        chi = jnp.where(lab == float(r), 3.0 * chi_t[r], chi)
    return lab, eps, chi


def source_and_lower(
    k, get_e, get_h, put_e, put_h, sv, labels, w, lo, hi, eps_t, chi_t, inv_power, s, mask_s, mask_h
):
    cz, cx, ny = labels.shape
    steps = sv.shape[0]
    base = (1 + 2 * (steps - 1 - k)) * 3 * cz
    plane = jnp.zeros((cx, ny), F32)
    for z in range(cz):
        lab, eps, chi = region(labels, lo, hi, eps_t, chi_t, z, cz)
        wz = jnp.concatenate([lo[13 * cz + z], w[z], hi[13 * cz + z]], 0) * inv_power
        along = jnp.zeros((cx, ny), F32)
        for c in range(3):
            slot = base + c * cz + z
            f = jnp.concatenate([lo[slot], sv[k, c, z].astype(F32), hi[slot]], 0)
            ec = get_e(c, z) + wz * f
            put_e(c, z, ec)
            sc = ec / (eps + chi * f * f)
            if mask_s is not None:
                sc = sc * mask_s
            s[c, z] = sc
            along = along + (sc * f)[PAD : PAD + cx]
        plane = plane + jnp.where(lab[PAD : PAD + cx] == 0.0, along, 0.0)
    for z in range(cz):
        sx, sy, sz = s[0, z], s[1, z], s[2, z]
        cx_ = sz - lower_y(sz) - sy
        cy_ = sx - sz + lower_x(sz)
        cz_ = sy - lower_x(sy) - sx + lower_y(sx)
        if z > 0:
            cx_ = cx_ + s[1, z - 1]
            cy_ = cy_ - s[0, z - 1]
        for c, curl in enumerate((cx_, cy_, cz_)):
            put_h(c, z, (get_h(c, z) - time_step * curl) * mask_h)
    return plane


def row_masks(tall, cx):
    row = lax.broadcasted_iota(jnp.int32, (tall, 128), 0)
    lat = lax.axis_index("lat")
    first = jnp.where(lat == 0, PAD, 0)
    last = jnp.where(lat == lax.axis_size("lat") - 1, PAD + cx, tall)
    mask_s = jnp.where(row >= first, 1.0, 0.0)
    mask_h = jnp.where(row < last, 1.0, 0.0)
    return mask_s, mask_h


def first_kernel(
    k, e, h, sv, labels, w, lo, hi, density, power, eps_t, chi_t, e_out, h_out, up, down, plane_out, deriv_out, s
):
    cz, cx, ny = labels.shape
    tall = e_out.shape[2]
    _, mask_h = row_masks(tall, cx)

    def get_e(c, z):
        return jnp.concatenate([lo[c * cz + z], e[c, z], hi[c * cz + z]], 0)

    def get_h(c, z):
        slot = (6 + c) * cz + z
        return jnp.concatenate([lo[slot], h[c, z], hi[slot]], 0)

    def put_e(c, z, v):
        e_out[c, z] = v

    def put_h(c, z, v):
        h_out[c, z] = v

    plane_out[...] = source_and_lower(
        k, get_e, get_h, put_e, put_h, sv, labels, w, lo, hi, eps_t, chi_t, power[k], s, None, mask_h
    )
    for c in range(2):
        up[c] = s[c, cz - 1]
        down[c] = h_out[c, 0]
    tiles = RADIUS // PAD
    padded = jnp.concatenate(
        [lo[14 * cz + t] for t in range(tiles)]
        + [density[...]]
        + [hi[14 * cz + t] for t in range(tiles)],
        0,
    )
    slope = jnp.tanh(sharpness * (smooth(padded, cx) - threshold))
    scale = jnp.tanh(jnp.full((1, ny), sharpness * threshold, F32)) + jnp.tanh(
        jnp.full((1, ny), sharpness * (1.0 - threshold), F32)
    )
    deriv_out[...] = sharpness * (1.0 - slope * slope) / scale


def finish_lower(h, get_h, recv_lo, recv_hi, up, mask_h):
    cz = h.shape[1]
    top = jnp.where(lax.axis_index("ha") == lax.axis_size("ha") - 1, 0.0, 1.0)
    low_x = h[0, 0] - time_step * (recv_lo[1] * mask_h)
    low_y = h[1, 0] + time_step * (recv_lo[0] * mask_h)
    above_x = (recv_hi[0] - time_step * up[1] * mask_h) * top
    above_y = (recv_hi[1] + time_step * up[0] * mask_h) * top
    return low_x, low_y, above_x, above_y


def upper_curl(hz_layer, above_x, above_y):
    hx, hy, hz = hz_layer
    curl_x = upper_y(hz) - hz - (above_y - hy)
    curl_y = above_x - hx - (upper_x(hz) - hz)
    curl_z = upper_x(hy) - hy - (upper_y(hx) - hx)
    return curl_x, curl_y, curl_z


def second_kernel(
    k, e, h, sv, labels, w, lo, hi, power, eps_t, chi_t, recv_lo, recv_hi, up1, plane1, deriv,
    e_out, h_out, up, down, product, s, e1,
):
    cz, cx, ny = labels.shape
    tall = e.shape[2]
    mask_s, mask_h = row_masks(tall, cx)
    low_x, low_y, above_x, above_y = finish_lower(h, None, recv_lo, recv_hi, up1, mask_h)

    def layer(c, z):
        if z == 0 and c < 2:
            return (low_x, low_y)[c]
        if z == cz:
            return (above_x, above_y)[c]
        return h[c, z]

    for z in range(cz):
        curls = upper_curl([layer(c, z) for c in range(3)], layer(0, z + 1), layer(1, z + 1))
        for c in range(3):
            e1[c, z] = e[c, z] + time_step * curls[c]

    def get_e(c, z):
        return e1[c, z]

    def put_e(c, z, v):
        e_out[c, z] = v

    def put_h(c, z, v):
        h_out[c, z] = v

    plane = source_and_lower(
        k, get_e, layer, put_e, put_h, sv, labels, w, lo, hi, eps_t, chi_t, power[k], s, mask_s, mask_h
    )
    product[...] = (plane1[...] + plane) * deriv[...]
    for c in range(2):
        up[c] = s[c, cz - 1]
        down[c] = h_out[c, 0]


def smooth_kernel(lo, mid, hi, out):
    out[...] = smooth(jnp.concatenate([lo[...], mid[...], hi[...]], 0), mid.shape[0])


def final_kernel(e, h, recv_lo, recv_hi, up, parts, e_out, h_out, grad):
    cz = h.shape[1]
    tall = e.shape[2]
    cx = e_out.shape[2]
    own = slice(PAD, PAD + cx)
    _, mask_h = row_masks(tall, cx)
    low_x, low_y, above_x, above_y = finish_lower(h, None, recv_lo, recv_hi, up, mask_h)

    def layer(c, z):
        if z == 0 and c < 2:
            return (low_x, low_y)[c]
        if z == cz:
            return (above_x, above_y)[c]
        return h[c, z]

    for z in range(cz):
        parts_h = [layer(c, z) for c in range(3)]
        curls = upper_curl(parts_h, layer(0, z + 1), layer(1, z + 1))
        for c in range(3):
            e_out[c, z] = (e[c, z] + time_step * curls[c])[own]
            h_out[c, z] = parts_h[c][own]
    total = parts[0]
    for i in range(1, parts.shape[0]):
        total = total + parts[i]
    grad[...] = total


def call(kernel, outs, specs, name, scratch=()):
    return pl.pallas_call(
        kernel,
        out_shape=[jax.ShapeDtypeStruct(o, F32) for o in outs],
        in_specs=specs,
        out_specs=[VMEM] * len(outs),
        scratch_shapes=[pltpu.VMEM(x, F32) for x in scratch],
        name=name,
    )


def body(
    adjoint_e, adjoint_h, saved_e, labels, eps_table, chi_table, density, mon_cells, mon_weight
):
    cz, cx, ny = labels.shape
    steps = saved_e.shape[0]
    tall = cx + 2 * PAD
    devices = lax.axis_size("lat") * lax.axis_size("ha")
    count_all = mon_cells.shape[0] * devices
    tiles = 14 * cz + RADIUS // PAD

    w, partial, nxt, prv = call(
        prepare_kernel,
        [(cz, cx, ny), (1, ny), (tiles, PAD, ny), (tiles, PAD, ny)],
        [VMEM] * 7,
        "prepare",
    )(
        adjoint_e,
        adjoint_h,
        saved_e,
        labels,
        density,
        mon_cells.reshape(1, -1),
        mon_weight.reshape(1, -1),
    )
    lo = shifted(nxt, "lat", 1)
    hi = shifted(prv, "lat", -1)
    spread = lax.all_to_all(
        jnp.broadcast_to(partial[None], (devices, 1, ny)), ("lat", "ha"), 0, 0
    )
    power = jnp.sum(spread, 0)[0, :steps] / count_all + epsilon
    inv_power = 1.0 / power

    field = (3, cz, tall, ny)
    edge = (2, tall, ny)
    e1, h1, up1, down1, plane1, deriv = call(
        lambda *refs: first_kernel(1, *refs),
        [field, field, edge, edge, (cx, ny), (cx, ny)],
        [VMEM] * 8 + [SMEM] * 3,
        "first",
        [field],
    )(adjoint_e, adjoint_h, saved_e, labels, w, lo, hi, density, inv_power, eps_table, chi_table)
    recv_lo = shifted(up1, "ha", 1)
    recv_hi = shifted(down1, "ha", -1)
    e0, h0, up0, down0, product = call(
        lambda *refs: second_kernel(0, *refs),
        [field, field, edge, edge, (cx, ny)],
        [VMEM] * 7 + [SMEM] * 3 + [VMEM] * 5,
        "second",
        [field, field],
    )(
        e1, h1, saved_e, labels, w, lo, hi, inv_power, eps_table, chi_table,
        recv_lo, recv_hi, up1, plane1, deriv,
    )
    below = shifted(product[cx - RADIUS :], "lat", 1)
    above = shifted(product[:RADIUS], "lat", -1)
    recv_lo = shifted(up0, "ha", 1)
    recv_hi = shifted(down0, "ha", -1)
    (local,) = call(smooth_kernel, [(cx, ny)], [VMEM] * 3, "smooth")(below, product, above)
    members = lax.axis_size("ha")
    parts = lax.all_to_all(jnp.broadcast_to(local[None], (members, cx, ny)), "ha", 0, 0)
    final_e, final_h, grad = call(
        final_kernel, [adjoint_e.shape, adjoint_h.shape, (cx, ny)], [VMEM] * 6, "final"
    )(e0, h0, recv_lo, recv_hi, up0, parts)
    return (final_e, final_h, grad)


def solution(mesh):
    return jax.shard_map(
        body,
        mesh=mesh,
        in_specs=(
            P(None, "ha", "lat", None),
            P(None, "ha", "lat", None),
            P(None, None, "ha", "lat", None),
            P("ha", "lat", None),
            P(),
            P(),
            P("lat", None),
            P(("lat", "ha")),
            P(("lat", "ha")),
        ),
        out_specs=(P(None, "ha", "lat", None), P(None, "ha", "lat", None), P("lat", None)),
        check_vma=False,
    )
```

```python
import jax
import jax.numpy as jnp
from jax import lax
from jax.experimental import pallas as pl
from jax.experimental.pallas import tpu as pltpu
from jax.sharding import PartitionSpec as P

RADIUS = 16
PAD = 8

sharpness = 8.0
threshold = 0.5
time_step = 0.5
epsilon = 1e-05

F32 = jnp.float32
VMEM = pl.BlockSpec(memory_space=pltpu.VMEM)
SMEM = pl.BlockSpec(memory_space=pltpu.SMEM)
PLANE = 72
SCOPED = 12 << 20


def inner_swap(value, axis):
    return lax.ppermute(value, axis, [(i, i ^ 1) for i in range(lax.axis_size(axis))])


def outer_swap(value, axis):
    count = lax.axis_size(axis)
    pairs = [(i, i + 1 if i % 2 else i - 1) for i in range(1, count - 1)]
    return lax.ppermute(value, axis, pairs)


def is_even(axis):
    return lax.axis_index(axis) % 2 == 0


def lower_y(v):
    lane = lax.broadcasted_iota(jnp.int32, v.shape, 1)
    return jnp.where(lane == 0, 0.0, pltpu.roll(v, 1, 1))


def upper_y(v):
    lane = lax.broadcasted_iota(jnp.int32, v.shape, 1)
    last = v.shape[1] - 1
    return jnp.where(lane == last, 0.0, pltpu.roll(v, last, 1))


def lower_x(v):
    return pltpu.roll(v, 1, 0)


def upper_x(v):
    return pltpu.roll(v, v.shape[0] - 1, 0)


def smooth(padded, rows):
    cols = padded.shape[1]
    tall = padded.shape[0]

    def cone(offset):
        return jnp.maximum(RADIUS + 1 - jnp.abs(offset), 0).astype(F32)

    a = lax.broadcasted_iota(jnp.int32, (cols, cols), 0)
    b = lax.broadcasted_iota(jnp.int32, (cols, cols), 1)
    across = jnp.dot(
        padded, cone(a - b), precision=lax.Precision.HIGHEST, preferred_element_type=F32
    )
    r = lax.broadcasted_iota(jnp.int32, (rows, tall), 0)
    s = lax.broadcasted_iota(jnp.int32, (rows, tall), 1)
    down = jnp.dot(
        cone(s - RADIUS - r), across, precision=lax.Precision.HIGHEST, preferred_element_type=F32
    )
    return down * (1.0 / (RADIUS + 1) ** 4)


def prepare_kernel(e, h, sv, labels, density, cells, weight, w_out, spread, inner, outer):
    cz, cx, ny = labels.shape
    count = cells.shape[1]
    even = is_even("lat")

    def send(slot, rows):
        last = rows[rows.shape[0] - PAD :]
        first = rows[:PAD]
        inner[slot] = jnp.where(even, last, first)
        outer[slot] = jnp.where(even, first, last)

    cell = cells[...]
    row = cell // ny
    col = cell % ny
    rows_hot = jnp.where(
        lax.broadcasted_iota(jnp.int32, (cz * cx, count), 0) == row, weight[...], 0.0
    )
    cols_hot = (lax.broadcasted_iota(jnp.int32, (ny, count), 0) == col).astype(F32)
    w = lax.dot_general(
        rows_hot,
        cols_hot,
        (((1,), (1,)), ((), ())),
        precision=lax.Precision.HIGHEST,
        preferred_element_type=F32,
    ).reshape(cz, cx, ny)
    w_out[...] = w
    steps = sv.shape[0]
    lane = lax.broadcasted_iota(jnp.int32, (1, ny), 1)
    packed = jnp.zeros((1, ny), F32)
    for k in range(steps):
        total = jnp.zeros((cx, ny), F32)
        for z in range(cz):
            square = jnp.zeros((cx, ny), F32)
            for c in range(3):
                f = sv[k, c, z].astype(F32)
                square = square + f * f
                send((1 + 2 * (steps - 1 - k)) * 3 * cz + c * cz + z, f)
            total = total + w[z] * square
        packed = jnp.where(lane == k, jnp.sum(total), packed)
    spread[...] = jnp.broadcast_to(packed[None], spread.shape)
    for z in range(cz):
        for c in range(3):
            send(c * cz + z, e.at[c, z])
            send((6 + c) * cz + z, h.at[c, z])
        send(12 * cz + z, labels[z].astype(F32))
        send(13 * cz + z, w[z])
    tiles = RADIUS // PAD
    for t in range(tiles):
        last = density[cx - RADIUS + t * PAD : cx - RADIUS + (t + 1) * PAD]
        first = density[t * PAD : (t + 1) * PAD]
        inner[14 * cz + t] = jnp.where(even, last, first)
        outer[14 * cz + t] = jnp.where(even, first, last)


class Sides:
    def __init__(self, inner, outer):
        self.inner, self.outer, self.even = inner, outer, is_even("lat")

    def both(self, slot):
        a, b = self.inner[slot], self.outer[slot]
        return jnp.where(self.even, b, a), jnp.where(self.even, a, b)

    def wrap(self, slot, mid):
        lo, hi = self.both(slot)
        return jnp.concatenate([lo, mid, hi], 0)


def derivative_kernel(density, inner, outer, out):
    cx, ny = density.shape
    tiles = RADIUS // PAD
    sides = Sides(inner, outer)
    base = inner.shape[0] - tiles
    pairs = [sides.both(base + t) for t in range(tiles)]
    padded = jnp.concatenate([p[0] for p in pairs] + [density[...]] + [p[1] for p in pairs], 0)
    slope = jnp.tanh(sharpness * (smooth(padded, cx) - threshold))
    scale = jnp.tanh(jnp.full((1, ny), sharpness * threshold, F32)) + jnp.tanh(
        jnp.full((1, ny), sharpness * (1.0 - threshold), F32)
    )
    out[...] = sharpness * (1.0 - slope * slope) / scale


def source_and_lower(
    k, get_e, get_h, put_e, put_h, sv, labels, w, sides, eps_t, chi_t, inv_power, s, mask_s, mask_h
):
    cz, cx, ny = labels.shape
    steps = sv.shape[0]
    base = (1 + 2 * (steps - 1 - k)) * 3 * cz
    plane = jnp.zeros((cx, ny), F32)
    for z in range(cz):
        lab = sides.wrap(12 * cz + z, labels[z].astype(F32))
        eps = jnp.full(lab.shape, eps_t[0], F32)
        chi = jnp.full(lab.shape, 3.0 * chi_t[0], F32)
        for r in range(1, eps_t.shape[0]):
            eps = jnp.where(lab == float(r), eps_t[r], eps)
            chi = jnp.where(lab == float(r), 3.0 * chi_t[r], chi)
        wz = sides.wrap(13 * cz + z, w[z]) * inv_power
        along = jnp.zeros((cx, ny), F32)
        for c in range(3):
            f = sides.wrap(base + c * cz + z, sv[k, c, z].astype(F32))
            ec = get_e(c, z) + wz * f
            put_e(c, z, ec)
            sc = ec / (eps + chi * f * f)
            if mask_s is not None:
                sc = sc * mask_s
            s[c, z] = sc
            along = along + (sc * f)[PAD : PAD + cx]
        plane = plane + jnp.where(lab[PAD : PAD + cx] == 0.0, along, 0.0)
    for z in range(cz):
        sx, sy, sz = s[0, z], s[1, z], s[2, z]
        curl_x = sz - lower_y(sz) - sy
        curl_y = sx - sz + lower_x(sz)
        curl_z = sy - lower_x(sy) - sx + lower_y(sx)
        if z > 0:
            curl_x = curl_x + s[1, z - 1]
            curl_y = curl_y - s[0, z - 1]
        for c, curl in enumerate((curl_x, curl_y, curl_z)):
            put_h(c, z, (get_h(c, z) - time_step * curl) * mask_h)
    return plane


def row_masks(tall, cx):
    row = lax.broadcasted_iota(jnp.int32, (tall, 128), 0)
    lat = lax.axis_index("lat")
    first = jnp.where(lat == 0, PAD, 0)
    last = jnp.where(lat == lax.axis_size("lat") - 1, PAD + cx, tall)
    mask_s = jnp.where(row >= first, 1.0, 0.0)
    mask_h = jnp.where(row < last, 1.0, 0.0)
    return mask_s, mask_h


def pack_edges(s, h, inner, outer):
    cz, tall = s.shape[1], s.shape[2]
    own = tall - 2 * PAD
    even = is_even("ha")
    row = lax.broadcasted_iota(jnp.int32, (PAD, s.shape[3]), 0)
    for c in range(2):
        up, down = s[c, cz - 1], h[c, 0]
        for start, a, b in (
            (0, up[PAD : PAD + own], down[PAD : PAD + own]),
            (
                own,
                jnp.where(row == PAD - 1, up[:PAD], up[PAD + own :]),
                jnp.where(row == PAD - 1, down[:PAD], down[PAD + own :]),
            ),
        ):
            at = pl.ds(c * PLANE + start, a.shape[0])
            inner[at] = jnp.where(even, a, b)
            outer[at] = jnp.where(even, b, a)


def unpack_edges(inner, outer):
    even = is_even("ha")
    below, above = [], []
    for c in range(2):
        a = inner[pl.ds(c * PLANE, PLANE)]
        b = outer[pl.ds(c * PLANE, PLANE)]
        own = PLANE - PAD
        for out, v in ((below, jnp.where(even, b, a)), (above, jnp.where(even, a, b))):
            out.append(jnp.concatenate([v[own:], v[:own], v[own:]], 0))
    return below, above


def completed(h, s_top, inner, outer, mask_h):
    cz = h.shape[1]
    below, above = unpack_edges(inner, outer)
    top = jnp.where(lax.axis_index("ha") == lax.axis_size("ha") - 1, 0.0, 1.0)
    low = (
        h[0, 0] - time_step * (below[1] * mask_h),
        h[1, 0] + time_step * (below[0] * mask_h),
    )
    high = (
        (above[0] - time_step * (s_top[1] * mask_h)) * top,
        (above[1] + time_step * (s_top[0] * mask_h)) * top,
    )

    def layer(c, z):
        if z == 0 and c < 2:
            return low[c]
        return high[c] if z == cz else h[c, z]

    return layer


def upper_curl(layer, z):
    hx, hy, hz = (layer(c, z) for c in range(3))
    above_x, above_y = layer(0, z + 1), layer(1, z + 1)
    return (
        upper_y(hz) - hz - (above_y - hy),
        above_x - hx - (upper_x(hz) - hz),
        upper_x(hy) - hy - (upper_y(hx) - hx),
    )


def first_kernel(
    k, count_all, e, h, sv, labels, w, inner, outer, spread, eps_t, chi_t,
    e_out, h_out, top_out, plane_out, inv_out, send_inner, send_outer, s,
):
    cz, cx, ny = labels.shape
    tall = e_out.shape[2]
    _, mask_h = row_masks(tall, cx)
    sides = Sides(inner, outer)
    inv = 1.0 / (jnp.sum(spread[...], 0) / count_all + epsilon)
    inv_out[...] = inv

    def get_e(c, z):
        return sides.wrap(c * cz + z, e[c, z])

    def get_h(c, z):
        return sides.wrap((6 + c) * cz + z, h[c, z])

    def put_e(c, z, v):
        e_out[c, z] = v

    def put_h(c, z, v):
        h_out[c, z] = v

    plane_out[...] = source_and_lower(
        k, get_e, get_h, put_e, put_h, sv, labels, w, sides, eps_t, chi_t,
        inv[:, k : k + 1], s, None, mask_h,
    )
    for c in range(2):
        top_out[c] = s[c, cz - 1]
    pack_edges(s, h_out, send_inner, send_outer)


def second_kernel(
    k, e, h, s_top, plane, inv, deriv, sv, labels, w, inner, outer, edge_inner, edge_outer, eps_t, chi_t,
    e_out, h_out, top_out, send_inner, send_outer, s, e1,
):
    cz, cx, ny = labels.shape
    tall = e.shape[2]
    mask_s, mask_h = row_masks(tall, cx)
    layer = completed(h, s_top, edge_inner, edge_outer, mask_h)
    for z in range(cz):
        curls = upper_curl(layer, z)
        for c in range(3):
            e1[c, z] = e[c, z] + time_step * curls[c]

    def get_e(c, z):
        return e1[c, z]

    def put_e(c, z, v):
        e_out[c, z] = v

    def put_h(c, z, v):
        h_out[c, z] = v

    total = plane[...] + source_and_lower(
        k, get_e, layer, put_e, put_h, sv, labels, w, Sides(inner, outer), eps_t, chi_t,
        inv[:, k : k + 1], s, mask_s, mask_h,
    )
    for c in range(2):
        top_out[c] = s[c, cz - 1]
    pack_edges(s, h_out, send_inner, send_outer)
    send_inner[pl.ds(2 * PLANE, cx)] = total * deriv[...]


def pair_kernel(mine, other, out):
    rows = out.shape[1]
    at = pl.ds(mine.shape[0] - rows, rows)
    both = mine[at] + other[at]
    for i in range(out.shape[0]):
        out[i] = both


def total_kernel(parts, out, inner, outer):
    total = parts[0]
    for i in range(1, parts.shape[0]):
        total = total + parts[i]
    out[...] = total
    even = is_even("lat")
    first, last = total[:RADIUS], total[total.shape[0] - RADIUS :]
    inner[...] = jnp.where(even, last, first)
    outer[...] = jnp.where(even, first, last)


def fields_kernel(e, h, s_top, inner, outer, e_out, h_out):
    cz = h.shape[1]
    tall = e.shape[2]
    cx = e_out.shape[2]
    own = slice(PAD, PAD + cx)
    _, mask_h = row_masks(tall, cx)
    layer = completed(h, s_top, inner, outer, mask_h)
    for z in range(cz):
        curls = upper_curl(layer, z)
        for c in range(3):
            e_out[c, z] = (e[c, z] + time_step * curls[c])[own]
            h_out[c, z] = layer(c, z)[own]


def smooth_kernel(mid, inner, outer, out):
    even = is_even("lat")
    a, b = inner[...], outer[...]
    padded = jnp.concatenate([jnp.where(even, b, a), mid[...], jnp.where(even, a, b)], 0)
    out[...] = smooth(padded, mid.shape[0])


def call(kernel, args, outs, name, tables=(), scratch=(), keep=True, held=True):
    if held:
        args = [pltpu.with_memory_space_constraint(a, pltpu.VMEM) for a in args]
    out = [pltpu.VMEM(o, F32) if keep else jax.ShapeDtypeStruct(o, F32) for o in outs]
    return pl.pallas_call(
        kernel,
        out_shape=out,
        in_specs=[VMEM] * len(args) + [SMEM] * len(tables),
        out_specs=[VMEM] * len(outs),
        scratch_shapes=[pltpu.VMEM(x, F32) for x in scratch],
        compiler_params=pltpu.CompilerParams(vmem_limit_bytes=SCOPED),
        name=name,
    )(*args, *tables)


def body(
    adjoint_e, adjoint_h, saved_e, labels, eps_table, chi_table, density, mon_cells, mon_weight
):
    cz, cx, ny = labels.shape
    tall = cx + 2 * PAD
    devices = lax.axis_size("lat") * lax.axis_size("ha")
    count_all = mon_cells.shape[0] * devices
    halo = (14 * cz + RADIUS // PAD, PAD, ny)
    tables = (eps_table, chi_table)

    w, partial, inner, outer = call(
        prepare_kernel,
        [
            adjoint_e,
            adjoint_h,
            saved_e,
            labels,
            density,
            mon_cells.reshape(1, -1),
            mon_weight.reshape(1, -1),
        ],
        [(cz, cx, ny), (devices, 1, ny), halo, halo],
        "prepare",
        held=False,
    )
    inner = inner_swap(inner, "lat")
    outer = outer_swap(outer, "lat")
    spread = lax.all_to_all(partial, ("lat", "ha"), 0, 0)

    field = (3, cz, tall, ny)
    edge = (2, tall, ny)
    e1, h1, top1, plane1, inv, edge_inner, edge_outer = call(
        lambda *refs: first_kernel(1, count_all, *refs),
        [adjoint_e, adjoint_h, saved_e, labels, w, inner, outer, spread],
        [field, field, edge, (cx, ny), (1, ny), (2 * PLANE, ny), (2 * PLANE, ny)],
        "first",
        tables,
        [field],
    )
    edge_inner = inner_swap(edge_inner, "ha")
    edge_outer = outer_swap(edge_outer, "ha")
    (deriv,) = call(derivative_kernel, [density, inner, outer], [(cx, ny)], "derivative")
    e0, h0, top0, mine, edge_outer = call(
        lambda *refs: second_kernel(0, *refs),
        [e1, h1, top1, plane1, inv, deriv, saved_e, labels, w, inner, outer, edge_inner, edge_outer],
        [field, field, edge, (2 * PLANE + cx, ny), (2 * PLANE, ny)],
        "second",
        tables,
        [field, field],
    )
    edge_inner = inner_swap(mine, "ha")
    edge_outer = outer_swap(edge_outer, "ha")
    members = lax.axis_size("ha") // 2
    (both,) = call(pair_kernel, [mine, edge_inner], [(members, cx, ny)], "pair")
    groups = [[2 * i + j for i in range(members)] for j in range(2)]
    parts = lax.all_to_all(both, "ha", 0, 0, axis_index_groups=groups)
    total, side_inner, side_outer = call(
        total_kernel, [parts], [(cx, ny), (RADIUS, ny), (RADIUS, ny)], "total"
    )
    side_inner = inner_swap(side_inner, "lat")
    side_outer = outer_swap(side_outer, "lat")
    final_e, final_h = call(
        fields_kernel,
        [e0, h0, top0, edge_inner, edge_outer],
        [adjoint_e.shape, adjoint_h.shape],
        "fields",
        keep=False,
    )
    (grad,) = call(smooth_kernel, [total, side_inner, side_outer], [(cx, ny)], "smooth", keep=False)
    return (final_e, final_h, grad)


def solution(mesh):
    return jax.shard_map(
        body,
        mesh=mesh,
        in_specs=(
            P(None, "ha", "lat", None),
            P(None, "ha", "lat", None),
            P(None, None, "ha", "lat", None),
            P("ha", "lat", None),
            P(),
            P(),
            P("lat", None),
            P(("lat", "ha")),
            P(("lat", "ha")),
        ),
        out_specs=(P(None, "ha", "lat", None), P(None, "ha", "lat", None), P("lat", None)),
        check_vma=False,
    )
```
